32 devices in a mesh: fsdp: 32 (over z, y, x, core).
Axes of the slice: x: 2, y: 2, z: 4, core: 2. Of those that a mesh axis runs over, the one named last changes fastest.
Arguments:
- tokens: bfloat16 [8192, 768], P('fsdp'), may hold values from -6 to 6
- ln1_gain: float32 [768], P('fsdp'), may hold values from 0.1 to 1.9
- ln1_bias: float32 [768], P('fsdp'), may hold values from -3 to 3
- w_qkv: bfloat16 [768, 2304], P('fsdp'), may hold values from -11 to 11
- bias_qv: float32 [1536], P('fsdp'), may hold values from -3 to 3
- w_out: bfloat16 [768, 768], P('fsdp'), may hold values from -0.625 to 0.625
- bias_out: float32 [768], P('fsdp'), may hold values from -3 to 3
- ln2_gain: float32 [768], P('fsdp'), may hold values from 0.1 to 1.9
- ln2_bias: float32 [768], P('fsdp'), may hold values from -3 to 3
- w_fc: bfloat16 [768, 3072], P('fsdp'), may hold values from -0.21875 to 0.21875
- bias_fc: float32 [3072], P('fsdp'), may hold values from -3 to 3
- w_proj: bfloat16 [3072, 768], P('fsdp'), may hold values from -0.109375 to 0.109375
- bias_proj: float32 [768], P('fsdp'), may hold values from -4 to 4
- cotangent: bfloat16 [8192, 768], P('fsdp'), may hold values from -6 to 6
Outputs:
- block_out: float32 [8192, 768], P('fsdp')
- grad_tokens: float32 [8192, 768], P('fsdp')
- grad_ln1_gain: float32 [768], P('fsdp')
- grad_ln1_bias: float32 [768], P('fsdp')
- grad_w_qkv: float32 [768, 2304], P('fsdp')
- grad_bias_qv: float32 [1536], P('fsdp')
- grad_w_out: float32 [768, 768], P('fsdp')
- grad_bias_out: float32 [768], P('fsdp')
- grad_ln2_gain: float32 [768], P('fsdp')
- grad_ln2_bias: float32 [768], P('fsdp')
- grad_w_fc: float32 [768, 3072], P('fsdp')
- grad_bias_fc: float32 [3072], P('fsdp')
- grad_w_proj: float32 [3072, 768], P('fsdp')
- grad_bias_proj: float32 [768], P('fsdp')
The draws below stay inside these ranges and needn't reach their ends.
All inputs are finite; a program needn't handle non-finite values.
Results may differ from the reference program's by a relative error of at most 0.025.
Values may be sent and summed in bfloat16 or wider, within the bound.
No kernel may reach another device: no remote copies, remote signals or barrier semaphores. Data moves between devices by JAX's collectives and lax.ppermute only.
A program may use at most 192 MiB of HBM per device.

```python
import jax
import jax.numpy as jnp
from jax import lax

D = 768
HEADS = 12
HEAD_DIM = 64
FF = 3072
LEN = 256
TOKENS = 8192


def draw_w_qkv(key, part):
    first = jax.random.fold_in(key, 0)
    base = jnp.clip(jax.random.normal(first, (D, 3 * D), jnp.float32), -4.0, 4.0) * D ** (-0.5)
    result = base
    return result.astype(jnp.bfloat16)


def block_levels(key, dims, cuts, low, top_value):
    factor_of = 1.0
    for dim, shards_of in cuts:
        steps = jax.random.uniform(jax.random.fold_in(jax.random.fold_in(key, 6), dim), (shards_of,), jnp.float32, low / len(cuts), top_value / len(cuts))
        factor_of = factor_of * jnp.repeat(jnp.exp(steps), dims[dim] // shards_of).reshape((-1,) + (1,) * (len(dims) - 1 - dim))
    return factor_of


def noise(key, extent, deviation, limit, pieces=(), kind=jnp.bfloat16):
    entries = deviation * jax.random.normal(key, extent, jnp.float32)
    if pieces:
        entries = entries * block_levels(key, extent, pieces, -0.22, 0.18)
    return jnp.clip(entries, -limit, limit).astype(kind)


def setup_inputs(seed: int = 0) -> dict:
    key_list = jax.random.split(jax.random.key(seed), 15)
    tokens = noise(key_list[0], (TOKENS, D), 1.0, 6.0, ((0, 32),))
    ln1_gain = jnp.clip(1.0 + 0.18 * jax.random.normal(key_list[1], (D,), jnp.float32), 0.1, 1.9)
    ln1_bias = noise(key_list[2], (D,), 0.5, 3.0, ((0, 32),), jnp.float32)
    w_qkv = draw_w_qkv(jax.random.fold_in(key_list[14], 71), 0)
    bias_qv = noise(key_list[4], (2 * D,), 0.5, 3.0, ((0, 32),), jnp.float32)
    w_out = noise(key_list[5], (D, D), (D // 8) ** -0.5, 0.625, ((0, 32),))
    bias_out = noise(key_list[6], (D,), 0.5, 3.0, ((0, 32),), jnp.float32)
    ln2_gain = jnp.clip(1.0 + 0.18 * jax.random.normal(key_list[7], (D,), jnp.float32), 0.1, 1.9)
    ln2_bias = noise(key_list[8], (D,), 0.5, 3.0, ((0, 32),), jnp.float32)
    w_fc = noise(key_list[9], (D, FF), D ** -0.5, 0.21875, ((0, 32),))
    bias_fc = noise(key_list[10], (FF,), 0.5, 3.0, ((0, 32),), jnp.float32)
    w_proj = noise(key_list[11], (FF, D), FF ** -0.5, 0.109375, ((0, 32),))
    bias_proj = noise(key_list[12], (D,), 1.0, 4.0, ((0, 32),), jnp.float32)
    cotangent = noise(key_list[13], (TOKENS, D), 1.0, 6.0, ((0, 32),))
    return {"tokens": tokens, "ln1_gain": ln1_gain, "ln1_bias": ln1_bias, "w_qkv": w_qkv, "bias_qv": bias_qv, "w_out": w_out, "bias_out": bias_out, "ln2_gain": ln2_gain, "ln2_bias": ln2_bias, "w_fc": w_fc, "bias_fc": bias_fc, "w_proj": w_proj, "bias_proj": bias_proj, "cotangent": cotangent}


GELU_COEF = 0.7978845608028654
EPSILON = 1e-05

def norm_forward(values, gain, shift):
    center = values - lax.optimization_barrier(jnp.mean(values, -1, keepdims=True))
    rstd = lax.rsqrt(lax.optimization_barrier(jnp.mean(center * center, -1, keepdims=True)) + EPSILON)
    normed = center * rstd
    return (normed, rstd, normed * gain + shift)

def norm_backward(grad_out, normed, rstd, gain):
    scaled = grad_out * gain
    return (scaled - lax.optimization_barrier(jnp.mean(scaled, -1, keepdims=True)) - normed * lax.optimization_barrier(jnp.mean(scaled * normed, -1, keepdims=True))) * rstd

def gelu_value(pre):
    inner = jnp.tanh(GELU_COEF * (pre + 0.044715 * pre * pre * pre))
    return 0.5 * pre * (1.0 + inner)

def gelu_slope(pre):
    inner = jnp.tanh(GELU_COEF * (pre + 0.044715 * pre * pre * pre))
    return 0.5 * (1.0 + inner) + 0.5 * pre * (1.0 - inner * inner) * GELU_COEF * (1.0 + 3.0 * 0.044715 * pre * pre)

def one_sequence(seq_in, seq_cot, params):
    g1, b1, wqkv, bqv, wout, bout, g2, b2, wfc, bfc, wproj, bproj = params
    width = D
    scale = HEAD_DIM ** (-0.5)
    inputs = seq_in.astype(jnp.float32)
    normed1, rstd1, ln1 = norm_forward(inputs, g1, b1)
    ln1_b = ln1.astype(jnp.bfloat16)
    mixed = jnp.dot(ln1_b, wqkv, preferred_element_type=jnp.float32)
    queries = (mixed[:, :width] + bqv[:width]).astype(jnp.bfloat16).reshape(LEN, HEADS, HEAD_DIM)
    keys_b = mixed[:, width:2 * width].astype(jnp.bfloat16).reshape(LEN, HEADS, HEAD_DIM)
    values_b = (mixed[:, 2 * width:] + bqv[width:]).astype(jnp.bfloat16).reshape(LEN, HEADS, HEAD_DIM)
    scores = jnp.einsum('qhd,khd->hqk', queries.astype(jnp.float32), keys_b.astype(jnp.float32)) * scale
    causal = jnp.arange(LEN)[:, None] >= jnp.arange(LEN)[None, :]
    scores = jnp.where(causal, scores, -1e+30)
    peak = lax.optimization_barrier(jnp.max(scores, -1, keepdims=True))
    lse = peak + jnp.log(lax.optimization_barrier(jnp.sum(jnp.exp(scores - peak), -1, keepdims=True)))
    probs = jnp.exp(scores - lse)
    probs_b = probs.astype(jnp.bfloat16)
    context = jnp.einsum('hqk,khd->qhd', probs_b.astype(jnp.float32), values_b.astype(jnp.float32))
    context_b = context.reshape(LEN, width).astype(jnp.bfloat16)
    resid = inputs + jnp.dot(context_b, wout, preferred_element_type=jnp.float32) + bout
    normed2, rstd2, ln2 = norm_forward(resid, g2, b2)
    ln2_b = ln2.astype(jnp.bfloat16)
    pre = jnp.dot(ln2_b, wfc, preferred_element_type=jnp.float32) + bfc
    hidden_b = gelu_value(pre).astype(jnp.bfloat16)
    block_out = resid + jnp.dot(hidden_b, wproj, preferred_element_type=jnp.float32) + bproj
    cot = seq_cot.astype(jnp.float32)
    d_bproj = lax.optimization_barrier(jnp.sum(cot, 0))
    d_wproj = jnp.dot(hidden_b.T, seq_cot, preferred_element_type=jnp.float32)
    grad_pre = jnp.dot(seq_cot, wproj.T, preferred_element_type=jnp.float32) * gelu_slope(pre)
    d_bfc = lax.optimization_barrier(jnp.sum(grad_pre, 0))
    grad_pre_b = grad_pre.astype(jnp.bfloat16)
    d_wfc = jnp.dot(ln2_b.T, grad_pre_b, preferred_element_type=jnp.float32)
    grad_ln2 = jnp.dot(grad_pre_b, wfc.T, preferred_element_type=jnp.float32)
    d_g2 = lax.optimization_barrier(jnp.sum(grad_ln2 * normed2, 0))
    d_b2 = lax.optimization_barrier(jnp.sum(grad_ln2, 0))
    grad_resid = cot + norm_backward(grad_ln2, normed2, rstd2, g2)
    grad_resid_b = grad_resid.astype(jnp.bfloat16)
    d_bout = lax.optimization_barrier(jnp.sum(grad_resid, 0))
    d_wout = jnp.dot(context_b.T, grad_resid_b, preferred_element_type=jnp.float32)
    grad_context = jnp.dot(grad_resid_b, wout.T, preferred_element_type=jnp.float32)
    grad_context_b = grad_context.astype(jnp.bfloat16).reshape(LEN, HEADS, HEAD_DIM).astype(jnp.float32)
    grad_probs = jnp.einsum('qhd,khd->hqk', grad_context_b, values_b.astype(jnp.float32))
    delta = lax.optimization_barrier(jnp.sum(probs * grad_probs, -1, keepdims=True))
    grad_scores = (probs * (grad_probs - delta) * scale).astype(jnp.bfloat16).astype(jnp.float32)
    grad_values = jnp.einsum('hqk,qhd->khd', probs_b.astype(jnp.float32), grad_context_b)
    grad_queries = jnp.einsum('hqk,khd->qhd', grad_scores, keys_b.astype(jnp.float32))
    grad_keys = jnp.einsum('hqk,qhd->khd', grad_scores, queries.astype(jnp.float32))
    grad_queries = grad_queries.reshape(LEN, width)
    grad_keys = grad_keys.reshape(LEN, width)
    grad_values = grad_values.reshape(LEN, width)
    d_bqv = jnp.concatenate([lax.optimization_barrier(jnp.sum(grad_queries, 0)), lax.optimization_barrier(jnp.sum(grad_values, 0))])
    grad_mixed = jnp.concatenate([grad_queries, grad_keys, grad_values], 1).astype(jnp.bfloat16)
    d_wqkv = jnp.dot(ln1_b.T, grad_mixed, preferred_element_type=jnp.float32)
    grad_ln1 = jnp.dot(grad_mixed, wqkv.T, preferred_element_type=jnp.float32)
    d_g1 = lax.optimization_barrier(jnp.sum(grad_ln1 * normed1, 0))
    d_b1 = lax.optimization_barrier(jnp.sum(grad_ln1, 0))
    grad_in = grad_resid + norm_backward(grad_ln1, normed1, rstd1, g1)
    grads = (d_g1, d_b1, d_wqkv, d_bqv, d_wout, d_bout, d_g2, d_b2, d_wfc, d_bfc, d_wproj, d_bproj)
    return (block_out, grad_in, grads)

def reference(tokens, ln1_gain, ln1_bias, w_qkv, bias_qv, w_out, bias_out, ln2_gain, ln2_bias, w_fc, bias_fc, w_proj, bias_proj, cotangent):
    params = (ln1_gain, ln1_bias, w_qkv, bias_qv, w_out, bias_out, ln2_gain, ln2_bias, w_fc, bias_fc, w_proj, bias_proj)
    count = tokens.shape[0] // LEN
    seq_in = tokens.reshape(count, LEN, D)
    seq_cot = cotangent.reshape(count, LEN, D)
    start = tuple((jnp.zeros(p.shape, jnp.float32) for p in params))

    def step(carry, item):
        out_seq, grad_seq, grads = one_sequence(item[0], item[1], params)
        return (tuple((a + b for a, b in zip(carry, grads))), (out_seq, grad_seq))
    totals, (outs_all, grads_all) = lax.scan(step, start, (seq_in, seq_cot))
    return (outs_all.reshape(count * LEN, D), grads_all.reshape(count * LEN, D)) + totals
```

```python
import jax
import jax.numpy as jnp
from jax import lax
from jax.sharding import PartitionSpec as P

HEADS = 12
HEAD_DIM = 64
LEN = 256


GELU_COEF = 0.7978845608028654
EPSILON = 1e-05


def norm_forward(values, gain, shift):
    center = values - jnp.mean(values, -1, keepdims=True)
    rstd = lax.rsqrt(jnp.mean(center * center, -1, keepdims=True) + EPSILON)
    normed = center * rstd
    return (normed, rstd, normed * gain + shift)


def norm_backward(grad_out, normed, rstd, gain):
    scaled = grad_out * gain
    return (
        scaled
        - jnp.mean(scaled, -1, keepdims=True)
        - normed * jnp.mean(scaled * normed, -1, keepdims=True)
    ) * rstd


def gelu_both(pre):
    inner = jnp.tanh(GELU_COEF * (pre + 0.044715 * pre * pre * pre))
    value = 0.5 * pre * (1.0 + inner)
    slope = 0.5 * (1.0 + inner) + 0.5 * pre * (1.0 - inner * inner) * GELU_COEF * (
        1.0 + 3.0 * 0.044715 * pre * pre
    )
    return value, slope


def swap(value, bit, count):
    return lax.ppermute(value, "fsdp", [(i, i ^ (1 << bit)) for i in range(count)])


def orders(count):
    bits = count.bit_length() - 1
    head = list(range(bits - 1, 2, -1))
    tail = [b for b in (1, 2) if b < bits]
    return head + tail + [0], head + tail[::-1] + [0]


def gather(shard, order, me, count):
    blocks = shard[None]
    done = []
    for bit in order:
        other = swap(blocks, bit, count)
        low = 1 << sum(b < bit for b in done)
        high = blocks.shape[0] // low
        shape = (high, low) + shard.shape
        upper = ((me >> bit) & 1) == 1
        own, other = blocks.reshape(shape), other.reshape(shape)
        pair = jnp.stack([jnp.where(upper, other, own), jnp.where(upper, own, other)], 1)
        blocks = pair.reshape((2 * high * low,) + shard.shape)
        done.append(bit)
    return blocks


def scatter(parts, order, me, count):
    left = list(range(count.bit_length() - 1))
    kind = parts.dtype
    block = parts.shape[1:]
    for bit in order[::-1]:
        low = 1 << sum(b < bit for b in left)
        high = parts.shape[0] // (2 * low)
        split = parts.reshape((high, 2, low) + block)
        mine = (me >> bit) & 1
        send = lax.dynamic_index_in_dim(split, 1 - mine, 1, keepdims=False)
        keep = lax.dynamic_index_in_dim(split, mine, 1, keepdims=False)
        got = swap(send, bit, count)
        total = keep.astype(jnp.float32) + got.astype(jnp.float32)
        left.remove(bit)
        parts = (total.astype(kind) if left else total).reshape((high * low,) + block)
    return parts[0]


def body(
    tokens,
    ln1_gain,
    ln1_bias,
    w_qkv,
    bias_qv,
    w_out,
    bias_out,
    ln2_gain,
    ln2_bias,
    w_fc,
    bias_fc,
    w_proj,
    bias_proj,
    cotangent,
    *,
    count,
):
    rows, width = tokens.shape
    me = lax.axis_index("fsdp")
    order_a, order_b = orders(count)
    small = (ln1_gain, ln1_bias, bias_qv, bias_out, ln2_gain, ln2_bias, bias_fc, bias_proj)
    sizes = [s.shape[0] for s in small]
    total = sum(sizes)
    padded = -(-total // 128) * 128

    def whole(shard):
        cols = shard.shape[1]
        half = cols // 2
        a = gather(shard[:, :half], order_a, me, count)
        b = gather(shard[:, half:], order_b, me, count)
        return [v.reshape(-1, half) for v in (a, b)]

    def shares(part_a, part_b):
        half = part_a.shape[1]
        a = scatter(part_a.reshape(count, -1, half), order_a, me, count)
        b = scatter(part_b.reshape(count, -1, half), order_b, me, count)
        return jnp.concatenate([a, b], 1)

    packed = jnp.concatenate(list(small) + [jnp.zeros((padded - total,), jnp.float32)])
    smalls = gather(packed.reshape(-1, 128), order_a, me, count).reshape(count, padded)
    params, at = [], 0
    for size in sizes:
        params.append(smalls[:, at : at + size].reshape(-1))
        at += size
    gain1, shift1, bqv, bout, gain2, shift2, bfc, bproj = params
    wqkv = jnp.concatenate(whole(w_qkv), 1)
    wout = jnp.concatenate(whole(w_out), 1)
    wfc = jnp.concatenate(whole(w_fc), 1)
    wproj = jnp.concatenate(whole(w_proj), 1)

    inputs = tokens.astype(jnp.float32)
    normed1, rstd1, ln1 = norm_forward(inputs, gain1, shift1)
    ln1_b = ln1.astype(jnp.bfloat16)
    mixed = jnp.dot(ln1_b, wqkv, preferred_element_type=jnp.float32)
    layout = (-1, LEN, HEADS, HEAD_DIM)
    queries = (mixed[:, :width] + bqv[:width]).astype(jnp.bfloat16).reshape(layout)
    keys_b = mixed[:, width : 2 * width].astype(jnp.bfloat16).reshape(layout)
    values_b = (mixed[:, 2 * width :] + bqv[width:]).astype(jnp.bfloat16).reshape(layout)
    scores = jnp.einsum(
        "sqhd,skhd->shqk", queries, keys_b, preferred_element_type=jnp.float32
    ) * HEAD_DIM ** (-0.5)
    causal = jnp.arange(LEN)[:, None] >= jnp.arange(LEN)[None, :]
    scores = jnp.where(causal, scores, -1e30)
    peak = jnp.max(scores, -1, keepdims=True)
    powers = jnp.exp(scores - peak)
    probs = powers / jnp.sum(powers, -1, keepdims=True)
    probs_b = probs.astype(jnp.bfloat16)
    context = jnp.einsum("shqk,skhd->sqhd", probs_b, values_b, preferred_element_type=jnp.float32)
    context_b = context.reshape(rows, width).astype(jnp.bfloat16)
    resid = inputs + jnp.dot(context_b, wout, preferred_element_type=jnp.float32) + bout
    normed2, rstd2, ln2 = norm_forward(resid, gain2, shift2)
    ln2_b = ln2.astype(jnp.bfloat16)
    pre = jnp.dot(ln2_b, wfc, preferred_element_type=jnp.float32) + bfc
    hidden, slope = gelu_both(pre)
    hidden_b = hidden.astype(jnp.bfloat16)

    def weight_grad(left, right):
        half = right.shape[1] // 2
        return shares(
            *(
                lax.dot_general(
                    left, part, (((0,), (0,)), ((), ())), preferred_element_type=jnp.float32
                ).astype(jnp.bfloat16)
                for part in (right[:, :half], right[:, half:])
            )
        )

    cot = cotangent.astype(jnp.float32)
    d_bproj = jnp.sum(cot, 0)
    d_wproj = weight_grad(hidden_b, cotangent)
    block_out = resid + jnp.dot(hidden_b, wproj, preferred_element_type=jnp.float32) + bproj
    grad_pre = jnp.dot(cotangent, wproj.T, preferred_element_type=jnp.float32) * slope
    d_bfc = jnp.sum(grad_pre, 0)
    grad_pre_b = grad_pre.astype(jnp.bfloat16)
    d_wfc = weight_grad(ln2_b, grad_pre_b)
    grad_ln2 = jnp.dot(grad_pre_b, wfc.T, preferred_element_type=jnp.float32)
    d_gain2 = jnp.sum(grad_ln2 * normed2, 0)
    d_shift2 = jnp.sum(grad_ln2, 0)
    grad_resid = cot + norm_backward(grad_ln2, normed2, rstd2, gain2)
    grad_resid_b = grad_resid.astype(jnp.bfloat16)
    d_bout = jnp.sum(grad_resid, 0)
    d_wout = weight_grad(context_b, grad_resid_b)
    grad_context = jnp.dot(grad_resid_b, wout.T, preferred_element_type=jnp.float32)
    grad_context_b = grad_context.astype(jnp.bfloat16).reshape(layout)
    grad_probs = jnp.einsum(
        "sqhd,skhd->shqk", grad_context_b, values_b, preferred_element_type=jnp.float32
    )
    delta = jnp.sum(probs * grad_probs, -1, keepdims=True)
    grad_scores = (probs * (grad_probs - delta) * HEAD_DIM ** (-0.5)).astype(jnp.bfloat16)
    grad_values = jnp.einsum(
        "shqk,sqhd->skhd", probs_b, grad_context_b, preferred_element_type=jnp.float32
    ).reshape(rows, width)
    grad_queries = jnp.einsum(
        "shqk,skhd->sqhd", grad_scores, keys_b, preferred_element_type=jnp.float32
    ).reshape(rows, width)
    grad_keys = jnp.einsum(
        "shqk,sqhd->skhd", grad_scores, queries, preferred_element_type=jnp.float32
    ).reshape(rows, width)
    d_bqv = jnp.concatenate([jnp.sum(grad_queries, 0), jnp.sum(grad_values, 0)])
    grad_mixed = jnp.concatenate([grad_queries, grad_keys, grad_values], 1).astype(jnp.bfloat16)
    d_wqkv = weight_grad(ln1_b, grad_mixed)
    grad_ln1 = jnp.dot(grad_mixed, wqkv.T, preferred_element_type=jnp.float32)
    d_gain1 = jnp.sum(grad_ln1 * normed1, 0)
    d_shift1 = jnp.sum(grad_ln1, 0)
    grad_tokens = grad_resid + norm_backward(grad_ln1, normed1, rstd1, gain1)

    grads = (d_gain1, d_shift1, d_bqv, d_bout, d_gain2, d_shift2, d_bfc, d_bproj)
    spread = [g.reshape(count, -1) for g in grads] + [jnp.zeros((count, padded - total), jnp.float32)]
    packed = jnp.concatenate(spread, 1).reshape(count, -1, 128)
    smalls = scatter(packed, order_a, me, count).reshape(padded)
    out, at = [], 0
    for size in sizes:
        out.append(smalls[at : at + size])
        at += size
    s_gain1, s_shift1, s_bqv, s_bout, s_gain2, s_shift2, s_bfc, s_bproj = out
    return (
        block_out,
        grad_tokens,
        s_gain1,
        s_shift1,
        d_wqkv,
        s_bqv,
        d_wout,
        s_bout,
        s_gain2,
        s_shift2,
        d_wfc,
        s_bfc,
        d_wproj,
        s_bproj,
    )


def solution(mesh):
    row, flat = P("fsdp", None), P("fsdp")
    count = mesh.shape["fsdp"]

    def step(*args):
        return body(*args, count=count)

    return jax.shard_map(
        step,
        mesh=mesh,
        in_specs=(row, flat, flat, row, flat, row, flat, flat, flat, row, flat, row, flat, row),
        out_specs=(row, row, flat, flat, row, flat, row, flat, flat, flat, row, flat, row, flat),
        check_vma=False,
    )
```
